256 devices in a mesh: range: 8 (over y, core), radial: 32 (over x, z).
Axes of the slice: x: 4, y: 4, z: 8, core: 2. Of those that a mesh axis runs over, the one named last changes fastest.
Arguments:
- field_start: bfloat16 [2, 2048, 1024], P(None, 'radial'), may hold values from -6 to 6
- phase_table: float32 [16, 1024], replicated, may hold values from -1.5 to 1.5
- profile_index: int32 [8, 2], replicated, may hold values from 0 to 15
- group_power: float32 [4], replicated, may hold values from 0.3 to 3
- group_slot: int32 [4], replicated, may hold values from 0 to 3, each once
- source_shift: int32 [8, 32], P('range'), may hold values from 0 to 31
- slot_sub: int32 [8, 32, 16], P('range'), may hold values from 0 to 3
- tile_count: int32 [8, 32], P('range'), may hold values from 1 to 16, as said below
- row_weights: bfloat16 [8, 32, 16, 16, 256], P('range', 'radial'), may hold values from -0.375 to 0.375
- col_weights: bfloat16 [8, 32, 16, 256, 256], P('range', 'radial'), may hold values from -0.375 to 0.375
Outputs:
- interference: float32 [8, 32, 256, 256], P('range', 'radial')
The draws below stay inside these ranges and needn't reach their ends.
Inputs may be any that keep to these rules, and one draw needn't show every extreme that they name: `tile_count`: in every slab some tile uses all 16 slots.
All inputs are finite; a program needn't handle non-finite values.
Results may differ from the reference program's by a relative error of at most 0.04.
Values may be sent and summed in bfloat16 or wider, within the bound.
A program may use at most 64 MiB of HBM per device.

```python
import math
import jax
import jax.numpy as jnp
from jax import lax

H = 1024
R_DEV = 64
STEPS = 2
VB = 128
SUB = 16
PIX = 256
K_MAX = 16
CAP = 2
GROUP_RADIALS = 512
PROFILES = 16
SLABS = 8
TILES = 32
RADIALS = 2048
GROUPS = 4
NSUB = 4
CHANNELS = 256
N_RADIAL = 32


def draw_tile_count(key, part):
    first_key, second_key = jax.random.split(jax.random.fold_in(key, 7))
    base = jax.random.randint(first_key, (SLABS, TILES), 1, K_MAX + 1)
    chosen = jax.random.randint(second_key, (SLABS,), 0, TILES)
    filled = jnp.arange(TILES)[None, :] == chosen[:, None]
    return jnp.where(filled, K_MAX, base).astype(jnp.int32)


def plant(values, stream_key, low, high):
    longest = values.shape.index(max(values.shape))
    spots = []
    for shift in (0, 1):
        where = [jax.random.randint(jax.random.fold_in(stream_key, axis), (), 0, length) for axis, length in enumerate(values.shape)]
        where[longest] = (where[longest] + shift) % values.shape[longest]
        spots.append(tuple(where))
    return values.at[spots[0]].set(low).at[spots[1]].set(high)


def block_levels(stream_key, extent, cuts, low, high):
    def one(position, parts):
        draws = jax.random.uniform(jax.random.fold_in(jax.random.fold_in(stream_key, 6), position), (parts,), jnp.float32, low / len(cuts), high / len(cuts))
        return jnp.repeat(jnp.exp(draws), extent[position] // parts).reshape((-1,) + (1,) * (len(extent) - position - 1))

    gain = one(*cuts[0])
    for cut in cuts[1:]:
        gain = gain * one(*cut)
    return gain


def normal_values(own_key, shape, spread, most, shards=(), kind=jnp.bfloat16):
    drawn = spread * jax.random.normal(own_key, shape, jnp.float32)
    if shards:
        drawn = drawn * block_levels(own_key, shape, shards, -0.22, 0.18)
    return jnp.clip(drawn, -most, most).astype(kind)


def setup_inputs(seed: int = 0) -> dict:
    keys = jax.random.split(jax.random.key(seed), 11)
    field_start = normal_values(keys[0], (2, RADIALS, H), 1.0, 6.0, ((1, 32),))
    phase_table = jnp.clip(jax.random.uniform(keys[1], (PROFILES, H), jnp.float32, -1.5, 1.5), -1.5, 1.5)
    profile_index = plant(jax.random.randint(keys[2], (SLABS, STEPS), 0, PROFILES), jax.random.fold_in(keys[2], 1), 0, PROFILES - 1).astype(jnp.int32)
    group_power = jnp.clip(jnp.exp(jax.random.uniform(keys[3], (GROUPS,), jnp.float32, math.log(0.3), math.log(3.0))), 0.3, 3.0)
    group_slot = jax.random.permutation(keys[4], GROUPS).astype(jnp.int32)
    source_shift = plant(jax.random.randint(keys[5], (SLABS, TILES), 0, TILES), jax.random.fold_in(keys[5], 1), 0, TILES - 1).astype(jnp.int32)
    slot_sub = plant(jax.random.randint(keys[6], (SLABS, TILES, K_MAX), 0, NSUB), jax.random.fold_in(keys[6], 1), 0, NSUB - 1).astype(jnp.int32)
    tile_count = draw_tile_count(jax.random.fold_in(keys[10], 71), 0)
    row_weights = normal_values(keys[8], (SLABS, TILES, K_MAX, SUB, PIX), (K_MAX * SUB) ** -0.5, 0.375, ((0, 8), (1, 32)))
    col_weights = normal_values(keys[9], (SLABS, TILES, K_MAX, CHANNELS, PIX), CHANNELS ** -0.5, 0.375, ((0, 8), (1, 32)))
    return {"field_start": field_start, "phase_table": phase_table, "profile_index": profile_index, "group_power": group_power, "group_slot": group_slot, "source_shift": source_shift, "slot_sub": slot_sub, "tile_count": tile_count, "row_weights": row_weights, "col_weights": col_weights}


spread_angle = 6.0
absorb_rate = 0.5

def dft_tables(height):
    index_row = jnp.arange(height, dtype=jnp.int32)
    product = index_row[:, None] * index_row[None, :] % height
    angle = 2.0 * math.pi / height * product.astype(jnp.float32)
    factor = 1.0 / math.sqrt(height)
    return ((jnp.cos(angle) * factor).astype(jnp.bfloat16), (jnp.sin(angle) * factor).astype(jnp.bfloat16))

def spectral_phase(height):
    index_row = jnp.arange(height, dtype=jnp.int32)
    folded = jnp.minimum(index_row, height - index_row).astype(jnp.float32)
    theta = -spread_angle * (2.0 * folded / height) ** 2
    return (jnp.cos(theta), jnp.sin(theta))

def absorber_profile(height):
    level = jnp.arange(height, dtype=jnp.int32).astype(jnp.float32)
    depth = jnp.maximum(0.0, (level - 0.9375 * height) / (0.0625 * height))
    return jnp.exp(-absorb_rate * depth * depth)

def march_slab(field, radial_gain, phases, cosine_table, sine_table, spectral_cos, spectral_sin, absorber, band):
    real_part = field[0]
    imag_part = field[1]
    row_total = real_part.shape[0]
    bands = []
    for step_index in range(phases.shape[0]):
        phase_cos = jnp.cos(phases[step_index])
        phase_sin = jnp.sin(phases[step_index])
        real_wide = real_part.astype(jnp.float32)
        imag_wide = imag_part.astype(jnp.float32)
        screened = jnp.concatenate([real_wide * phase_cos - imag_wide * phase_sin, real_wide * phase_sin + imag_wide * phase_cos], 0).astype(jnp.bfloat16)
        with_cos = jnp.dot(screened, cosine_table, preferred_element_type=jnp.float32)
        with_sin = jnp.dot(screened, sine_table, preferred_element_type=jnp.float32)
        spec_real = with_cos[:row_total] + with_sin[row_total:]
        spec_imag = with_cos[row_total:] - with_sin[:row_total]
        moved = jnp.concatenate([spec_real * spectral_cos - spec_imag * spectral_sin, spec_real * spectral_sin + spec_imag * spectral_cos], 0).astype(jnp.bfloat16)
        back_cos = jnp.dot(moved, cosine_table, preferred_element_type=jnp.float32)
        back_sin = jnp.dot(moved, sine_table, preferred_element_type=jnp.float32)
        real_part = ((back_cos[:row_total] - back_sin[row_total:]) * absorber).astype(jnp.bfloat16)
        imag_part = ((back_cos[row_total:] + back_sin[:row_total]) * absorber).astype(jnp.bfloat16)
        real_low = real_part.astype(jnp.float32)[:, :band]
        imag_low = imag_part.astype(jnp.float32)[:, :band]
        bands.append((radial_gain[:, None] * (real_low * real_low + imag_low * imag_low)).astype(jnp.bfloat16))
    return (jnp.stack([real_part, imag_part]), jnp.concatenate(bands, axis=1))

def reference(field_start, phase_table, profile_index, group_power, group_slot, source_shift, slot_sub, tile_count, row_weights, col_weights):
    cosine_table, sine_table = dft_tables(H)
    spectral_cos, spectral_sin = spectral_phase(H)
    absorber = absorber_profile(H)
    radial_ids = jnp.arange(RADIALS, dtype=jnp.int32)
    radial_gain = group_power[group_slot[radial_ids // GROUP_RADIALS]]
    field = field_start
    polar_list = []
    for slab_index in range(SLABS):
        phases = phase_table[profile_index[slab_index]]
        field, polar_block = march_slab(field, radial_gain, phases, cosine_table, sine_table, spectral_cos, spectral_sin, absorber, VB)
        polar_list.append(polar_block)
    polar = jnp.stack(polar_list)

    def one_slab(operands):
        polar_block, shift_row, sub_rows, count_row, row_part, col_part = operands
        slot_ids = jnp.arange(K_MAX, dtype=jnp.int32)
        tile_ids = jnp.arange(TILES, dtype=jnp.int32)
        source = (tile_ids[:, None] + shift_row[:, None] + (slot_ids // CAP)[None, :]) % N_RADIAL
        row_index = source[:, :, None] * R_DEV + sub_rows[:, :, None] * SUB + jnp.arange(SUB, dtype=jnp.int32)[None, None, :]
        pieces = polar_block[row_index]
        is_live = slot_ids[None, :] < count_row[:, None]
        pieces = jnp.where(is_live[:, :, None, None], pieces, jnp.zeros_like(pieces))
        mixed = jnp.einsum('tksc,tkcp->tksp', pieces.astype(jnp.float32), col_part.astype(jnp.float32)).astype(jnp.bfloat16)
        return jnp.einsum('tksp,tksq->tpq', row_part.astype(jnp.float32), mixed.astype(jnp.float32))
    return lax.map(one_slab, (polar, source_shift, slot_sub, tile_count, row_weights, col_weights))
```

```python
import functools

import jax
import jax.numpy as jnp
import ml_dtypes
import numpy as np
from jax import lax
from jax.experimental import pallas as pl
from jax.experimental.pallas import tpu as pltpu
from jax.sharding import PartitionSpec as P

MESH = pl.DeviceIdType.MESH
F32 = jnp.float32
BF16 = jnp.bfloat16

H = 1024
CHUNK = 256
VB = 128
SUB = 16
PIX = 256
K_MAX = 16
SLABS = 8
NX = 4
NZ = 8
GROUP_DEVICES = 8

spread_angle = 6.0
absorb_rate = 0.5


def propagator_blocks():
    order = np.arange(H)
    folded = np.minimum(order, H - order)
    theta = -spread_angle * (2.0 * folded / H) ** 2
    lagged = np.fft.ifft(np.exp(1j * theta))
    place = np.arange(CHUNK)
    lag = place[None, :] - place[:, None]
    turn = (1.0, -1j, -1.0, 1j)
    blocks = []
    for j in range(4):
        block = sum(turn[j * c % 4] * lagged[(CHUNK * c + lag) % H] for c in range(4)) / 4
        blocks.append(np.concatenate([block.real, block.imag], axis=1))
    return np.stack(blocks).astype(ml_dtypes.bfloat16)


def absorber_tail():
    level = np.arange(H - 128, H)
    depth = np.maximum(0.0, (level - 0.9375 * H) / (0.0625 * H))
    return np.exp(-absorb_rate * depth * depth).astype(np.float32).reshape(1, 128)


def cos_sin(angle):
    sq = angle * angle
    cosine = F32(-1.0 / 87178291200)
    for value in (1.0 / 479001600, -1.0 / 3628800, 1.0 / 40320, -1.0 / 720, 1.0 / 24, -1.0 / 2, 1.0):
        cosine = cosine * sq + F32(value)
    sine = F32(1.0 / 6227020800)
    for value in (-1.0 / 39916800, 1.0 / 362880, -1.0 / 5040, 1.0 / 120, -1.0 / 6, 1.0):
        sine = sine * sq + F32(value)
    return cosine, sine * angle


def kernel(
    field_hbm,
    phase_hbm,
    profile_hbm,
    power_hbm,
    slot_hbm,
    shift_hbm,
    sub_hbm,
    count_hbm,
    row_hbm,
    col_hbm,
    block_hbm,
    tail_hbm,
    out_ref,
    field_in,
    phase_in,
    cos_tab,
    sin_tab,
    blocks,
    tail,
    row_in,
    col_in,
    march,
    sent,
    gathered,
    picked,
    landed,
    row_turned,
    mixed,
    profile,
    power,
    slot,
    shift,
    sub_of,
    count,
    in_sem,
    send_sem,
    recv_sem,
    send2_sem,
    recv2_sem,
):
    n_own = lax.axis_index("range")
    r_own = lax.axis_index("radial")
    pair = n_own // 4
    part = n_own % 4
    x_own = r_own // NZ
    z_own = r_own % NZ

    first_row = pl.multiple_of(part * SUB, SUB)
    loads = [
        pltpu.make_async_copy(field_hbm.at[:, pl.ds(first_row, SUB), :], field_in, in_sem.at[0]),
        pltpu.make_async_copy(phase_hbm, phase_in, in_sem.at[1]),
        pltpu.make_async_copy(profile_hbm, profile, in_sem.at[2]),
        pltpu.make_async_copy(power_hbm, power, in_sem.at[3]),
        pltpu.make_async_copy(slot_hbm, slot, in_sem.at[4]),
        pltpu.make_async_copy(block_hbm, blocks, in_sem.at[5]),
        pltpu.make_async_copy(tail_hbm, tail, in_sem.at[6]),
        pltpu.make_async_copy(shift_hbm, shift, in_sem.at[7]),
        pltpu.make_async_copy(sub_hbm, sub_of, in_sem.at[8]),
        pltpu.make_async_copy(count_hbm, count, in_sem.at[9]),
        pltpu.make_async_copy(row_hbm.at[0, 0], row_in, in_sem.at[10]),
        pltpu.make_async_copy(col_hbm.at[0, 0], col_in, in_sem.at[11]),
    ]
    for load in loads:
        load.start()

    barrier = pltpu.get_barrier_semaphore()
    for dp in range(4):
        for dx in range(NX):
            if dp or dx:
                peer = (pair * 4 + (part + dp) % 4, (x_own + dx) % NX * NZ + z_own)
                pl.semaphore_signal(barrier, inc=1, device_id=peer, device_id_type=MESH)
    for dz in range(1, NZ):
        peer = (n_own, x_own * NZ + (z_own + dz) % NZ)
        pl.semaphore_signal(barrier, inc=1, device_id=peer, device_id_type=MESH)

    for load in loads[:7]:
        load.wait()
    cosine, sine = cos_sin(phase_in[...])
    cos_tab[...] = cosine
    sin_tab[...] = sine
    march[...] = field_in[...].astype(F32)
    gain = power[slot[x_own // (GROUP_DEVICES // NZ)]]

    def one_step(re, im, number, step):
        row = profile[number, step]
        cosine = cos_tab[pl.ds(row, 1), :]
        sine = sin_tab[pl.ds(row, 1), :]
        sr = re * cosine - im * sine
        si = re * sine + im * cosine
        r0, r1, r2, r3 = (sr[:, a * CHUNK : (a + 1) * CHUNK] for a in range(4))
        i0, i1, i2, i3 = (si[:, a * CHUNK : (a + 1) * CHUNK] for a in range(4))
        er, ei, fr, fi = r0 + r2, i0 + i2, r1 + r3, i1 + i3
        gr, gi, hr, hi = r0 - r2, i0 - i2, r1 - r3, i1 - i3
        entering = ((er + fr, ei + fi), (gr + hi, gi - hr), (er - fr, ei - fi), (gr - hi, gi + hr))
        leaving = []
        for j, (vr, vi) in enumerate(entering):
            both = jnp.concatenate([vr, vi], axis=0).astype(BF16)
            product = jnp.dot(both, blocks[j], preferred_element_type=F32)
            leaving.append(
                (
                    product[:SUB, :CHUNK] - product[SUB:, CHUNK:],
                    product[:SUB, CHUNK:] + product[SUB:, :CHUNK],
                )
            )
        (y0r, y0i), (y1r, y1i), (y2r, y2i), (y3r, y3i) = leaving
        pr, pi, qr, qi = y0r + y2r, y0i + y2i, y0r - y2r, y0i - y2i
        tr, ti, dr, di = y1r + y3r, y1i + y3i, y1r - y3r, y1i - y3i
        re = jnp.concatenate([pr + tr, qr - di, pr - tr, qr + di], axis=1)
        im = jnp.concatenate([pi + ti, qi + dr, pi - ti, qi - dr], axis=1)
        top = tail[...]
        re = jnp.concatenate([re[:, : H - 128], re[:, H - 128 :] * top], axis=1)
        im = jnp.concatenate([im[:, : H - 128], im[:, H - 128 :] * top], axis=1)
        return re, im

    def warm(number, carry):
        re, im = march[0], march[1]
        for step in range(2):
            re, im = one_step(re, im, number, step)
        march[0] = re
        march[1] = im
        return carry

    lax.fori_loop(0, pair * 4, warm, 0)

    pl.semaphore_wait(barrier, 4 * NX - 1 + NZ - 1)

    def block_copy(j, dx):
        return pltpu.make_async_remote_copy(
            src_ref=sent.at[j],
            dst_ref=gathered.at[x_own, part],
            send_sem=send_sem.at[j, dx],
            recv_sem=recv_sem.at[x_own, part],
            device_id=(pair * 4 + j, (x_own + dx) % NX * NZ + z_own),
            device_id_type=MESH,
        )

    def live(j, carry):
        re, im = march[0], march[1]
        bands = []
        for step in range(2):
            re, im = one_step(re, im, pair * 4 + j, step)
            low_re, low_im = re[:, :VB], im[:, :VB]
            bands.append(gain * (low_re * low_re + low_im * low_im))
        polar = jnp.concatenate(bands, axis=1).astype(BF16)
        sent[j] = polar

        @pl.when(j == part)
        def _():
            gathered[x_own, part] = polar

        march[0] = re
        march[1] = im
        for dx in range(1, NX):
            block_copy(j, dx).start()

        @pl.when(j != part)
        def _():
            block_copy(j, 0).start()

        return carry

    lax.fori_loop(0, 4, live, 0)

    for load in loads[7:]:
        load.wait()
    own_shift = shift[0, r_own]

    def slot_pair(dz):
        return lax.rem(2 * NZ - dz + NZ * 4 - own_shift, NZ)

    rows = []
    for dz in range(NZ):
        first = 2 * slot_pair(dz)
        rows.append(row_in[first])
        rows.append(row_in[first + 1])
    row_turned[...] = jnp.concatenate(rows, axis=0).T

    def arrived(xs, ps):
        return pltpu.make_async_remote_copy(
            src_ref=sent.at[0],
            dst_ref=gathered.at[xs, ps],
            send_sem=send_sem.at[0, 0],
            recv_sem=recv_sem.at[xs, ps],
            device_id=(n_own, r_own),
            device_id_type=MESH,
        )

    for dp in range(4):
        for dx in range(NX):
            if dp or dx:
                arrived((x_own + dx) % NX, (part + dp) % 4).wait_recv()

    def pick_copy(dz):
        return pltpu.make_async_remote_copy(
            src_ref=picked.at[dz],
            dst_ref=landed.at[dz],
            send_sem=send2_sem.at[dz],
            recv_sem=recv2_sem.at[dz],
            device_id=(n_own, x_own * NZ + (z_own + dz) % NZ),
            device_id_type=MESH,
        )

    for dz in (4, 3, 5, 2, 6, 1, 7, 0):
        tile = x_own * NZ + (z_own + dz) % NZ
        begin = tile + shift[0, tile]
        ahead = lax.rem(z_own + 64 - lax.rem(begin, NZ), NZ)
        source = lax.rem(lax.rem(begin + ahead, NX * NZ) // NZ, NX)
        for i in range(2):
            k = 2 * ahead + i
            block = gathered[source, sub_of[0, tile, k]]
            block = jnp.where(k < count[0, tile], block, jnp.zeros_like(block))
            if dz:
                picked[dz, i] = block
            else:
                landed[0, i] = block
        if dz:
            pick_copy(dz).start()

    for dz in (0, 1, 7, 2, 6, 3, 5, 4):
        if dz:
            pick_copy(dz).wait_recv()
        first = 2 * slot_pair(dz)
        for i in range(2):
            product = jnp.dot(landed[dz, i], col_in[first + i], preferred_element_type=F32)
            mixed[dz * 2 * SUB + i * SUB : dz * 2 * SUB + (i + 1) * SUB, :] = product.astype(BF16)
    out_ref[0, 0] = jnp.dot(row_turned[...], mixed[...], preferred_element_type=F32)

    def sends_done(j, carry):
        for dx in range(1, NX):
            block_copy(j, dx).wait_send()

        @pl.when(j != part)
        def _():
            block_copy(j, 0).wait_send()

        return carry

    lax.fori_loop(0, 4, sends_done, 0)
    for dz in range(1, NZ):
        pick_copy(dz).wait_send()


def per_device(
    field_start,
    phase_table,
    profile_index,
    group_power,
    group_slot,
    source_shift,
    slot_sub,
    tile_count,
    row_weights,
    col_weights,
):
    dma = pltpu.SemaphoreType.DMA
    anywhere = pl.BlockSpec(memory_space=pl.ANY)
    return pl.pallas_call(
        kernel,
        out_shape=jax.ShapeDtypeStruct((1, 1, PIX, PIX), F32),
        in_specs=[anywhere] * 12,
        out_specs=pl.BlockSpec(memory_space=pltpu.VMEM),
        scratch_shapes=[
            pltpu.VMEM((2, SUB, H), BF16),
            pltpu.VMEM(phase_table.shape, F32),
            pltpu.VMEM(phase_table.shape, F32),
            pltpu.VMEM(phase_table.shape, F32),
            pltpu.VMEM((4, CHUNK, 2 * CHUNK), BF16),
            pltpu.VMEM((1, 128), F32),
            pltpu.VMEM((K_MAX, SUB, PIX), BF16),
            pltpu.VMEM((K_MAX, 2 * VB, PIX), BF16),
            pltpu.VMEM((2, SUB, H), F32),
            pltpu.VMEM((4, SUB, 2 * VB), BF16),
            pltpu.VMEM((NX, 4, SUB, 2 * VB), BF16),
            pltpu.VMEM((NZ, 2, SUB, 2 * VB), BF16),
            pltpu.VMEM((NZ, 2, SUB, 2 * VB), BF16),
            pltpu.VMEM((PIX, K_MAX * SUB), BF16),
            pltpu.VMEM((K_MAX * SUB, PIX), BF16),
            pltpu.SMEM(profile_index.shape, jnp.int32),
            pltpu.SMEM(group_power.shape, F32),
            pltpu.SMEM(group_slot.shape, jnp.int32),
            pltpu.SMEM(source_shift.shape, jnp.int32),
            pltpu.SMEM(slot_sub.shape, jnp.int32),
            pltpu.SMEM(tile_count.shape, jnp.int32),
            dma((12,)),
            dma((4, NX)),
            dma((NX, 4)),
            dma((NZ,)),
            dma((NZ,)),
        ],
        compiler_params=pltpu.CompilerParams(collective_id=0, has_side_effects=True),
    )(
        field_start,
        phase_table,
        profile_index,
        group_power,
        group_slot,
        source_shift,
        slot_sub,
        tile_count,
        row_weights,
        col_weights,
        jnp.asarray(propagator_blocks()),
        jnp.asarray(absorber_tail()),
    )


def solution(mesh):
    return jax.shard_map(
        per_device,
        mesh=mesh,
        in_specs=(
            P(None, "radial", None),
            P(),
            P(),
            P(),
            P(),
            P("range", None),
            P("range", None, None),
            P("range", None),
            P("range", "radial", None, None, None),
            P("range", "radial", None, None, None),
        ),
        out_specs=P("range", "radial", None, None),
        check_vma=False,
    )
```

```python
import functools

import jax
import jax.numpy as jnp
import ml_dtypes
import numpy as np
from jax import lax
from jax.experimental import pallas as pl
from jax.experimental.pallas import tpu as pltpu
from jax.sharding import PartitionSpec as P

MESH = pl.DeviceIdType.MESH
F32 = jnp.float32
BF16 = jnp.bfloat16

H = 1024
CHUNK = 256
VB = 128
SUB = 16
PIX = 256
K_MAX = 16
SLABS = 8
NX = 4
NZ = 8
GROUP_DEVICES = 8

spread_angle = 6.0
absorb_rate = 0.5


def propagator_blocks():
    order = np.arange(H)
    folded = np.minimum(order, H - order)
    theta = -spread_angle * (2.0 * folded / H) ** 2
    lagged = np.fft.ifft(np.exp(1j * theta))
    place = np.arange(CHUNK)
    lag = place[None, :] - place[:, None]
    turn = (1.0, -1j, -1.0, 1j)
    blocks = []
    for j in range(4):
        block = sum(turn[j * c % 4] * lagged[(CHUNK * c + lag) % H] for c in range(4)) / 4
        blocks.append(np.concatenate([block.real, block.imag], axis=1))
    return np.stack(blocks).astype(ml_dtypes.bfloat16)


def absorber_tail():
    level = np.arange(H - 128, H)
    depth = np.maximum(0.0, (level - 0.9375 * H) / (0.0625 * H))
    return np.exp(-absorb_rate * depth * depth).astype(np.float32).reshape(1, 128)


def cos_sin(angle):
    sq = angle * angle
    cosine = F32(-1.0 / 87178291200)
    for value in (1.0 / 479001600, -1.0 / 3628800, 1.0 / 40320, -1.0 / 720, 1.0 / 24, -1.0 / 2, 1.0):
        cosine = cosine * sq + F32(value)
    sine = F32(1.0 / 6227020800)
    for value in (-1.0 / 39916800, 1.0 / 362880, -1.0 / 5040, 1.0 / 120, -1.0 / 6, 1.0):
        sine = sine * sq + F32(value)
    return cosine, sine * angle


def kernel(
    field_hbm,
    phase_hbm,
    profile_hbm,
    power_hbm,
    slot_hbm,
    shift_hbm,
    sub_hbm,
    count_hbm,
    row_hbm,
    col_hbm,
    block_hbm,
    tail_hbm,
    out_ref,
    field_in,
    phase_in,
    cos_tab,
    sin_tab,
    blocks,
    tail,
    row_in,
    col_in,
    march,
    sent,
    gathered,
    picked,
    landed,
    row_turned,
    mixed,
    profile,
    power,
    slot,
    shift,
    sub_of,
    count,
    in_sem,
    send_sem,
    recv_sem,
    send2_sem,
    recv2_sem,
):
    n_own = lax.axis_index("range")
    r_own = lax.axis_index("radial")
    pair = n_own // 4
    part = n_own % 4
    x_own = r_own // NZ
    z_own = r_own % NZ

    first_row = pl.multiple_of(part * SUB, SUB)
    loads = [
        pltpu.make_async_copy(field_hbm.at[:, pl.ds(first_row, SUB), :], field_in, in_sem.at[0]),
        pltpu.make_async_copy(phase_hbm, phase_in, in_sem.at[1]),
        pltpu.make_async_copy(profile_hbm, profile, in_sem.at[2]),
        pltpu.make_async_copy(power_hbm, power, in_sem.at[3]),
        pltpu.make_async_copy(slot_hbm, slot, in_sem.at[4]),
        pltpu.make_async_copy(block_hbm, blocks, in_sem.at[5]),
        pltpu.make_async_copy(tail_hbm, tail, in_sem.at[6]),
        pltpu.make_async_copy(shift_hbm, shift, in_sem.at[7]),
        pltpu.make_async_copy(sub_hbm, sub_of, in_sem.at[8]),
        pltpu.make_async_copy(count_hbm, count, in_sem.at[9]),
        pltpu.make_async_copy(row_hbm.at[0, 0], row_in, in_sem.at[10]),
        pltpu.make_async_copy(col_hbm.at[0, 0], col_in, in_sem.at[11]),
    ]
    for load in loads:
        load.start()

    barrier = pltpu.get_barrier_semaphore()
    for dp in range(4):
        for dx in range(NX):
            if dp or dx:
                peer = (pair * 4 + (part + dp) % 4, (x_own + dx) % NX * NZ + z_own)
                pl.semaphore_signal(barrier, inc=1, device_id=peer, device_id_type=MESH)
    for dz in range(1, NZ):
        peer = (n_own, x_own * NZ + (z_own + dz) % NZ)
        pl.semaphore_signal(barrier, inc=1, device_id=peer, device_id_type=MESH)

    for load in loads[:7]:
        load.wait()
    cosine, sine = cos_sin(phase_in[...])
    cos_tab[...] = cosine
    sin_tab[...] = sine
    march[...] = field_in[...].astype(F32)
    gain = power[slot[x_own // (GROUP_DEVICES // NZ)]]

    def one_step(re, im, number, step):
        row = profile[step, number]
        cosine = cos_tab[pl.ds(row, 1), :]
        sine = sin_tab[pl.ds(row, 1), :]
        sr = re * cosine - im * sine
        si = re * sine + im * cosine
        r0, r1, r2, r3 = (sr[:, a * CHUNK : (a + 1) * CHUNK] for a in range(4))
        i0, i1, i2, i3 = (si[:, a * CHUNK : (a + 1) * CHUNK] for a in range(4))
        er, ei, fr, fi = r0 + r2, i0 + i2, r1 + r3, i1 + i3
        gr, gi, hr, hi = r0 - r2, i0 - i2, r1 - r3, i1 - i3
        entering = ((er + fr, ei + fi), (gr + hi, gi - hr), (er - fr, ei - fi), (gr - hi, gi + hr))
        leaving = []
        for j, (vr, vi) in enumerate(entering):
            both = jnp.concatenate([vr, vi], axis=0).astype(BF16)
            product = jnp.dot(both, blocks[j], preferred_element_type=F32)
            leaving.append(
                (
                    product[:SUB, :CHUNK] - product[SUB:, CHUNK:],
                    product[:SUB, CHUNK:] + product[SUB:, :CHUNK],
                )
            )
        (y0r, y0i), (y1r, y1i), (y2r, y2i), (y3r, y3i) = leaving
        pr, pi, qr, qi = y0r + y2r, y0i + y2i, y0r - y2r, y0i - y2i
        tr, ti, dr, di = y1r + y3r, y1i + y3i, y1r - y3r, y1i - y3i
        re = jnp.concatenate([pr + tr, qr - di, pr - tr, qr + di], axis=1)
        im = jnp.concatenate([pi + ti, qi + dr, pi - ti, qi - dr], axis=1)
        top = tail[...]
        re = jnp.concatenate([re[:, : H - 128], re[:, H - 128 :] * top], axis=1)
        im = jnp.concatenate([im[:, : H - 128], im[:, H - 128 :] * top], axis=1)
        return re, im

    def warm(number, carry):
        re, im = march[0], march[1]
        for step in range(2):
            re, im = one_step(re, im, number, step)
        march[0] = re
        march[1] = im
        return carry

    lax.fori_loop(0, pair * 4, warm, 0)

    pl.semaphore_wait(barrier, 4 * NX - 1 + NZ - 1)

    def block_copy(j, dx):
        return pltpu.make_async_remote_copy(
            src_ref=sent.at[j],
            dst_ref=gathered.at[x_own, part],
            send_sem=send_sem.at[j, dx],
            recv_sem=recv_sem.at[x_own, part],
            device_id=(pair * 4 + j, (x_own + dx) % NX * NZ + z_own),
            device_id_type=MESH,
        )

    def live(j, carry):
        re, im = march[0], march[1]
        bands = []
        for step in range(2):
            re, im = one_step(re, im, pair * 4 + j, step)
            low_re, low_im = re[:, :VB], im[:, :VB]
            bands.append(gain * (low_re * low_re + low_im * low_im))
        polar = jnp.concatenate(bands, axis=1).astype(BF16)
        sent[j] = polar

        @pl.when(j == part)
        def _():
            gathered[x_own, part] = polar

        march[0] = re
        march[1] = im
        for dx in range(1, NX):
            block_copy(j, dx).start()

        @pl.when(j != part)
        def _():
            block_copy(j, 0).start()

        return carry

    lax.fori_loop(0, 4, live, 0)

    for load in loads[7:]:
        load.wait()
    own_shift = shift[0, r_own]

    def slot_pair(dz):
        return lax.rem(2 * NZ - dz + NZ * 4 - own_shift, NZ)

    rows = []
    for dz in range(NZ):
        first = 2 * slot_pair(dz)
        rows.append(row_in[first])
        rows.append(row_in[first + 1])
    row_turned[...] = jnp.concatenate(rows, axis=0).T

    def arrived(xs, ps):
        return pltpu.make_async_remote_copy(
            src_ref=sent.at[0],
            dst_ref=gathered.at[xs, ps],
            send_sem=send_sem.at[0, 0],
            recv_sem=recv_sem.at[xs, ps],
            device_id=(n_own, r_own),
            device_id_type=MESH,
        )

    for dp in range(4):
        for dx in range(NX):
            if dp or dx:
                arrived((x_own + dx) % NX, (part + dp) % 4).wait_recv()

    def pick_copy(dz):
        return pltpu.make_async_remote_copy(
            src_ref=picked.at[dz],
            dst_ref=landed.at[dz],
            send_sem=send2_sem.at[dz],
            recv_sem=recv2_sem.at[dz],
            device_id=(n_own, x_own * NZ + (z_own + dz) % NZ),
            device_id_type=MESH,
        )

    for dz in (4, 3, 5, 2, 6, 1, 7, 0):
        tile = x_own * NZ + (z_own + dz) % NZ
        begin = tile + shift[0, tile]
        ahead = lax.rem(z_own + 64 - lax.rem(begin, NZ), NZ)
        source = lax.rem(lax.rem(begin + ahead, NX * NZ) // NZ, NX)
        for i in range(2):
            k = 2 * ahead + i
            block = gathered[source, sub_of[0, k, tile]]
            block = jnp.where(k < count[0, tile], block, jnp.zeros_like(block))
            if dz:
                picked[dz, i] = block
            else:
                landed[0, i] = block
        if dz:
            pick_copy(dz).start()

    for dz in (0, 1, 7, 2, 6, 3, 5, 4):
        if dz:
            pick_copy(dz).wait_recv()
        first = 2 * slot_pair(dz)
        for i in range(2):
            product = jnp.dot(landed[dz, i], col_in[first + i], preferred_element_type=F32)
            mixed[dz * 2 * SUB + i * SUB : dz * 2 * SUB + (i + 1) * SUB, :] = product.astype(BF16)
    out_ref[0, 0] = jnp.dot(row_turned[...], mixed[...], preferred_element_type=F32)

    def sends_done(j, carry):
        for dx in range(1, NX):
            block_copy(j, dx).wait_send()

        @pl.when(j != part)
        def _():
            block_copy(j, 0).wait_send()

        return carry

    lax.fori_loop(0, 4, sends_done, 0)
    for dz in range(1, NZ):
        pick_copy(dz).wait_send()


def per_device(
    field_start,
    phase_table,
    profile_index,
    group_power,
    group_slot,
    source_shift,
    slot_sub,
    tile_count,
    row_weights,
    col_weights,
):
    dma = pltpu.SemaphoreType.DMA
    anywhere = pl.BlockSpec(memory_space=pl.ANY)
    return pl.pallas_call(
        kernel,
        out_shape=pltpu.VMEM((1, 1, PIX, PIX), F32),
        in_specs=[anywhere] * 12,
        out_specs=pl.BlockSpec(memory_space=pltpu.VMEM),
        scratch_shapes=[
            pltpu.VMEM((2, SUB, H), BF16),
            pltpu.VMEM(phase_table.shape, F32),
            pltpu.VMEM(phase_table.shape, F32),
            pltpu.VMEM(phase_table.shape, F32),
            pltpu.VMEM((4, CHUNK, 2 * CHUNK), BF16),
            pltpu.VMEM((1, 128), F32),
            pltpu.VMEM((K_MAX, SUB, PIX), BF16),
            pltpu.VMEM((K_MAX, 2 * VB, PIX), BF16),
            pltpu.VMEM((2, SUB, H), F32),
            pltpu.VMEM((4, SUB, 2 * VB), BF16),
            pltpu.VMEM((NX, 4, SUB, 2 * VB), BF16),
            pltpu.VMEM((NZ, 2, SUB, 2 * VB), BF16),
            pltpu.VMEM((NZ, 2, SUB, 2 * VB), BF16),
            pltpu.VMEM((PIX, K_MAX * SUB), BF16),
            pltpu.VMEM((K_MAX * SUB, PIX), BF16),
            pltpu.SMEM(profile_index.shape[::-1], jnp.int32),
            pltpu.SMEM(group_power.shape, F32),
            pltpu.SMEM(group_slot.shape, jnp.int32),
            pltpu.SMEM(source_shift.shape, jnp.int32),
            pltpu.SMEM((1, K_MAX, NX * NZ), jnp.int32),
            pltpu.SMEM(tile_count.shape, jnp.int32),
            dma((12,)),
            dma((4, NX)),
            dma((NX, 4)),
            dma((NZ,)),
            dma((NZ,)),
        ],
        compiler_params=pltpu.CompilerParams(collective_id=0, has_side_effects=True),
    )(
        field_start,
        phase_table,
        profile_index.T,
        group_power,
        group_slot,
        source_shift,
        slot_sub.transpose(0, 2, 1),
        tile_count,
        row_weights,
        col_weights,
        jnp.asarray(propagator_blocks()),
        jnp.asarray(absorber_tail()),
    )


def solution(mesh):
    return jax.shard_map(
        per_device,
        mesh=mesh,
        in_specs=(
            P(None, "radial", None),
            P(),
            P(),
            P(),
            P(),
            P("range", None),
            P("range", None, None),
            P("range", None),
            P("range", "radial", None, None, None),
            P("range", "radial", None, None, None),
        ),
        out_specs=P("range", "radial", None, None),
        check_vma=False,
    )
```
